768 devices in a mesh: cd: 48 (over x_lo, z, core), ij: 16 (over y, x_hi).
Axes of the slice: x: 4 (x_hi: 2, x_lo: 2; x = x_hi * 2 + x_lo), y: 8, z: 12, core: 2. Of those that a mesh axis runs over, the one named last changes fastest.
Arguments:
- left_factor: bfloat16 [24576, 4096], P('cd'), may hold values from -6 to 6
- right_factor: bfloat16 [4096, 4, 1024], P(None, None, 'ij'), may hold values from -0.09375 to 0.09375
- amplitudes: float32 [192, 1152, 1024], P('ij', 'cd'), may hold values from -0.015625 to 0.015625
- heights: int32 [48], P('cd'), may hold values from 256 to 512, as said below
- owner_map: int32 [48, 512, 1], P('cd'), may hold values from 0 to 47; in each aligned block of 512 rows (0 to 511, 512 to 1023, ..., all dimensions but the last counted through in order) at most 16 rows name the same one
- row_site: int32 [48, 512], P('cd'), may hold values from 0 to 23
Outputs:
- residual: float32 [768], P(('ij', 'cd'))
The draws below stay inside these ranges and needn't reach their ends.
Inputs may be any that keep to these rules, and one draw needn't show every extreme that they name: `heights`: some former has exactly 512 live rows. `owner_map`: within the 512 rows of one former no tile is named more than 16 times, and that bound is reached.
All inputs are finite; a program needn't handle non-finite values.
Results may differ from the reference program's by a relative error of at most 0.0028.
Values may be sent and summed in bfloat16 or wider, within the bound.
No kernel may reach another device: no remote copies, remote signals or barrier semaphores. Data moves between devices by JAX's collectives and lax.ppermute only.
A program may use at most 32 MiB of HBM per device.

```python
import math
import jax
import jax.numpy as jnp
import numpy as np
from jax import lax

NAUX = 4096
VIRT = 1024
NB = 4
C_TILE = 24
HMAX = 512
CAP = 16
NC = 1152
NIJ = 192
FORMED = 24576
N_CD = 48


def draw_heights(key, part):
    first, second = jax.random.split(jax.random.fold_in(key, 11))
    drawn = jax.random.randint(first, (N_CD,), HMAX // 2, HMAX + 1)
    tallest = jax.random.randint(second, (), 0, N_CD)
    return jnp.where(jnp.arange(N_CD) == tallest, HMAX, drawn).astype(jnp.int32)


def with_ends(values, own_key, smallest, largest):
    longest = values.shape.index(max(values.shape))
    spots = []
    for shift in (0, 1):
        where = [jax.random.randint(jax.random.fold_in(own_key, axis), (), 0, length) for axis, length in enumerate(values.shape)]
        where[longest] = (where[longest] + shift) % values.shape[longest]
        spots.append(tuple(where))
    return values.at[spots[0]].set(smallest).at[spots[1]].set(largest)


def block_scale(key, shape, cuts, least, top_value):
    def one(axis_at, parts):
        draws = jax.random.uniform(jax.random.fold_in(jax.random.fold_in(key, 6), axis_at), (parts,), jnp.float32, least / len(cuts), top_value / len(cuts))
        return jnp.repeat(jnp.exp(draws), shape[axis_at] // parts).reshape((-1,) + (1,) * (len(shape) - axis_at - 1))

    gain = one(*cuts[0])
    for cut in cuts[1:]:
        gain = gain * one(*cut)
    return gain


def shared_out(stream_key, own, number, rows, amount, top, reach, slope):
    ranking = jax.random.permutation(stream_key, amount)
    heavy_load, usual = load_shares(amount, rows * top, reach, slope, True), load_shares(amount, rows * top, reach, slope, False)
    places = jnp.arange(amount)

    def named(lengths, turn):
        used = int((lengths > 0).sum())
        fixed = max(1, used // 4)
        passed = fixed + (places - fixed + turn * (used - fixed)) % max(1, amount - fixed)
        return jnp.zeros((amount,), jnp.int32).at[ranking[jnp.where(places < fixed, places, passed)]].set(jnp.asarray(lengths, jnp.int32))

    lengths = jnp.where(number % 4 == 0, named(heavy_load, number // 4), named(usual, number - number // 4 - 1))
    mixed = jax.random.permutation(jax.random.fold_in(own, 3), amount)
    giver, taker = mixed[0:amount // 2 * 2:2], mixed[1:amount // 2 * 2:2]
    room = jnp.minimum(lengths[giver] - 1, reach - lengths[taker]) // 2
    room = jnp.where((giver == ranking[0]) | (taker == ranking[0]) | (lengths[taker] == 0), 0, jnp.maximum(room, 0))
    passed = jax.random.randint(jax.random.fold_in(own, 4), (amount // 2,), 0, 1 << 20) % (room + 1)
    lengths = lengths.at[giver].add(-passed).at[taker].add(passed)
    members = jnp.searchsorted(jnp.cumsum(lengths), jnp.arange(rows * top), side="right").astype(jnp.int32)
    grid = members.reshape(top, rows).T
    grid = grid[jax.random.permutation(jax.random.fold_in(own, 1), rows)]
    turn = jax.random.randint(jax.random.fold_in(own, 2), (rows, 1), 0, top)
    return jnp.take_along_axis(grid, (jnp.arange(top)[None, :] + turn) % top, axis=1)


def load_shares(count, total, most, slope, full):
    portions = [(1 << 20) // math.isqrt(standing ** slope) + 1 for standing in range(1, count + 1)]
    largest = most if full else min(most, max(-(-total // count), total * portions[0] // sum(portions)))
    least = 1 if total - largest >= count - 1 else 0
    counts, rest = [largest] + [least] * (count - 1), total - largest - least * (count - 1)
    while rest > 0:
        free = [i for i in range(1, count) if counts[i] < largest] or [i for i in range(1, count) if counts[i] < most]
        mass, budget = sum([portions[i] for i in free]), rest
        for i in free:
            extra = min(most - counts[i], max(1, budget * portions[i] // mass), rest)
            counts[i] = counts[i] + extra
            rest = rest - extra
    return np.array(counts)


def normal_values(own_key, shape, deviation, most, cuts=(), kind=jnp.bfloat16):
    result = jax.random.normal(own_key, shape, jnp.float32) * deviation
    if len(cuts) > 0:
        result = block_scale(own_key, shape, cuts, -0.22, 0.18) * result
    return jnp.clip(result, min=-most, max=most).astype(kind)


def setup_inputs(seed: int = 0) -> dict:
    keys = jax.random.split(jax.random.key(seed), 7)
    left_factor = normal_values(keys[0], (FORMED, NAUX), 1.0, 6.0, ((0, 48),))
    right_factor = normal_values(keys[1], (NAUX, NB, VIRT), NAUX ** -0.5, 0.09375, ((2, 16),))
    amplitudes = normal_values(keys[2], (NIJ, NC, VIRT), (NC * VIRT // 8) ** -0.5, 0.015625, ((0, 16), (1, 48)), jnp.float32)
    heights = draw_heights(jax.random.fold_in(keys[6], 71), 0)
    owner_map_keys = jax.random.split(jax.random.fold_in(keys[4], 1), N_CD * HMAX // HMAX)
    owner_map_turns = jax.random.permutation(jax.random.fold_in(keys[4], 3), N_CD * HMAX // HMAX)
    owner_map = jax.vmap(lambda own, number: shared_out(jax.random.fold_in(keys[4], 2), own, number, HMAX, N_CD, 1, CAP, 2))(owner_map_keys, owner_map_turns).reshape((N_CD, HMAX, 1))
    row_site = with_ends(jax.random.randint(keys[5], (N_CD, HMAX), 0, C_TILE), jax.random.fold_in(keys[5], 1), 0, C_TILE - 1).astype(jnp.int32)
    return dict(left_factor=left_factor, right_factor=right_factor, amplitudes=amplitudes, heights=heights, owner_map=owner_map, row_site=row_site)


def reference(left_factor, right_factor, amplitudes, heights, owner_map, row_site):
    formers = heights.shape[0]
    rows = left_factor.shape[0] // formers
    panel = jnp.dot(left_factor, right_factor.reshape(right_factor.shape[0], -1), preferred_element_type=jnp.float32)
    position = jnp.arange(rows, dtype=jnp.int32)
    live = (position[None, :] < heights[:, None]).reshape(-1)
    panel = jnp.where(live[:, None], panel, 0.0).astype(jnp.bfloat16).astype(jnp.float32)
    orbital = (owner_map[:, :, 0] * C_TILE + row_site).reshape(-1).astype(jnp.int32)
    sums = jax.ops.segment_sum(panel, orbital, num_segments=NC)
    sums = sums.reshape(NC, NB, VIRT)
    residual = jnp.einsum("icd,cbd->ib", amplitudes.astype(jnp.float32), sums, precision=lax.Precision.HIGHEST)
    return residual.reshape(-1)
```

```python
import jax
import jax.numpy as jnp
from jax import lax
from jax.experimental import pallas as pl
from jax.experimental.pallas import tpu as pltpu
from jax.sharding import PartitionSpec as P

SLOTS = 16
LANES = 128
KSTEPS = 8
QBITS = 14


def form_kernel(heights, place, owners, sites, left, right, out, acc, dispatch, tags):
    step = pl.program_id(0)
    rows = left.shape[0]
    formers = out.shape[0]
    slots = formers * SLOTS

    @pl.when(step == 0)
    def _():
        acc[...] = jnp.zeros_like(acc)
        live = lax.broadcasted_iota(jnp.int32, (1, rows), 1) < heights[0]
        owner = jnp.where(live, owners[...], -1)
        hits = lax.broadcasted_iota(jnp.int32, (formers, rows), 0) == owner
        hits_f = jnp.where(hits, 1.0, 0.0)
        upto = lax.broadcasted_iota(jnp.int32, (rows, rows), 0) <= lax.broadcasted_iota(
            jnp.int32, (rows, rows), 1
        )
        upto = jnp.where(upto, 1.0, 0.0).astype(jnp.bfloat16)
        count = jnp.dot(hits_f.astype(jnp.bfloat16), upto, preferred_element_type=jnp.float32)
        within = jnp.sum(hits_f * count, axis=0, keepdims=True).astype(jnp.int32) - 1
        target = jnp.where(live, owner * SLOTS + within, -1)
        chosen = lax.broadcasted_iota(jnp.int32, (slots, rows), 0) == target
        dispatch[...] = jnp.where(chosen, 1.0, 0.0).astype(jnp.bfloat16)
        lane = within + (place[0] % (LANES // SLOTS)) * SLOTS
        at_lane = lax.broadcasted_iota(jnp.int32, (LANES, rows), 0) == lane
        at_lane = jnp.where(at_lane, 1.0, 0.0).astype(jnp.bfloat16)
        tagged = hits_f * (sites[...] + 1).astype(jnp.float32)
        tags[...] = lax.dot_general(
            tagged.astype(jnp.bfloat16),
            at_lane,
            (((1,), (1,)), ((), ())),
            preferred_element_type=jnp.float32,
        )

    acc[...] += lax.dot_general(
        left[...], right[...], (((1,), (1,)), ((), ())), preferred_element_type=jnp.float32
    )

    @pl.when(step == KSTEPS - 1)
    def _():
        panel = acc[...].astype(jnp.bfloat16)
        moved = jnp.dot(dispatch[...], panel, preferred_element_type=jnp.float32)
        moved = moved.astype(jnp.bfloat16)
        width = moved.shape[1] // LANES
        for part in range(width):
            piece = moved[:, part * LANES : (part + 1) * LANES]
            out[:, part * SLOTS : (part + 1) * SLOTS, :] = piece.reshape(formers, SLOTS, LANES)
        tag = jnp.broadcast_to(tags[...][:, None, :], (formers, 8, LANES))
        out[:, width * SLOTS : width * SLOTS + 8, :] = tag.astype(jnp.bfloat16)


def form(heights, place, owners, sites, left, right, formers):
    rows, naux = left.shape
    cols = right.shape[0]
    block = naux // KSTEPS
    depth = cols // LANES * SLOTS + 8
    return pl.pallas_call(
        form_kernel,
        grid=(KSTEPS,),
        in_specs=[
            pl.BlockSpec(memory_space=pltpu.SMEM),
            pl.BlockSpec(memory_space=pltpu.SMEM),
            pl.BlockSpec((1, rows), lambda k: (0, 0)),
            pl.BlockSpec((1, rows), lambda k: (0, 0)),
            pl.BlockSpec((rows, block), lambda k: (0, k)),
            pl.BlockSpec((cols, block), lambda k: (0, k)),
        ],
        out_specs=pl.BlockSpec((formers, depth, LANES), lambda k: (0, 0, 0)),
        out_shape=jax.ShapeDtypeStruct((formers, depth, LANES), jnp.bfloat16),
        scratch_shapes=[
            pltpu.VMEM((rows, cols), jnp.float32),
            pltpu.VMEM((formers * SLOTS, rows), jnp.bfloat16),
            pltpu.VMEM((formers, LANES), jnp.float32),
        ],
        compiler_params=pltpu.CompilerParams(dimension_semantics=("arbitrary",)),
        name="form",
    )(heights, place, owners, sites, left, right)


def combine_kernel(arrived, out):
    formers = arrived.shape[0]
    copies, depth, cols = out.shape
    tile = depth - 8
    width = cols // LANES
    group = LANES // SLOTS
    tags = arrived[:, width * SLOTS : width * SLOTS + 8, :].astype(jnp.float32)
    site = lax.broadcasted_iota(jnp.int32, (tile, LANES), 0).astype(jnp.float32) + 1.0
    pickers = []
    for g in range(formers // group):
        tag = jnp.sum(tags[g * group : (g + 1) * group], axis=0)
        tag = jnp.concatenate([tag] * (tile // 8), axis=0)
        pickers.append(jnp.where(tag == site, 1.0, 0.0).astype(jnp.bfloat16))
    picker = jnp.concatenate(pickers, axis=1)
    for part in range(width):
        rows = arrived[:, part * SLOTS : (part + 1) * SLOTS, :].reshape(formers * SLOTS, LANES)
        sums = jnp.dot(picker, rows, preferred_element_type=jnp.float32)
        top = jnp.maximum(jnp.max(jnp.abs(sums), axis=0, keepdims=True), 2.0**-100)
        power = jnp.ceil(jnp.log(top) * 1.4426950408889634)
        coded = jnp.round(sums * jnp.exp2(QBITS - power))
        whole = jnp.concatenate([coded, jnp.broadcast_to(power, (8, LANES))], axis=0)
        whole = whole.astype(jnp.int32).astype(jnp.int16)
        for copy in range(copies):
            out[copy, :, part * LANES : (part + 1) * LANES] = whole


def combine(arrived, copies, tile, cols):
    return pl.pallas_call(
        combine_kernel,
        out_shape=jax.ShapeDtypeStruct((copies, tile + 8, cols), jnp.int16),
        name="combine",
    )(arrived)


def contract_kernel(amplitudes, pieces, out, sums, ends):
    pairs, tile, _ = amplitudes.shape
    count, _, cols = pieces.shape
    dpiece = LANES // 2
    bwidth = cols // dpiece
    low = lax.broadcasted_iota(jnp.int32, (tile, LANES), 1) < dpiece
    for two in range(count // 2):
        both = []
        for j in (2 * two, 2 * two + 1):
            whole = pieces[j].astype(jnp.int32).astype(jnp.float32)
            both.append(whole[:tile] * jnp.exp2(whole[tile : tile + 1] - QBITS))
        for half in range(cols // LANES):
            a, b = [v[:, half * LANES : (half + 1) * LANES] for v in both]
            span = slice(two * LANES, (two + 1) * LANES)
            sums[2 * half, :, span] = jnp.where(low, a, pltpu.roll(b, dpiece, 1))
            sums[2 * half + 1, :, span] = jnp.where(low, pltpu.roll(a, dpiece, 1), b)
    some = 6
    for first in range(0, pairs, some):
        totals = [[jnp.zeros((8, LANES), jnp.float32) for _ in range(bwidth)] for _ in range(some)]
        for c in range(0, tile, 8):
            for d in range(0, amplitudes.shape[2], LANES):
                s = [sums[b, c : c + 8, d : d + LANES] for b in range(bwidth)]
                for i in range(some):
                    t = amplitudes[first + i, c : c + 8, d : d + LANES]
                    for b in range(bwidth):
                        totals[i][b] = totals[i][b] + t * s[b]
        for i in range(some):
            for b in range(bwidth):
                at = (first + i) * bwidth + b
                ends[at : at + 1, :] = jnp.sum(totals[i][b], axis=0, keepdims=True)
    total = jnp.sum(ends[...], axis=1, keepdims=True)
    out[...] = jnp.broadcast_to(total, ends.shape)[:, None, :]


def contract(amplitudes, pieces):
    pairs, tile, virt = amplitudes.shape
    bwidth = pieces.shape[2] * 2 // LANES
    return pl.pallas_call(
        contract_kernel,
        out_shape=jax.ShapeDtypeStruct((pairs * bwidth, 1, LANES), jnp.float32),
        scratch_shapes=[
            pltpu.VMEM((bwidth, tile, virt), jnp.float32),
            pltpu.VMEM((pairs * bwidth, LANES), jnp.float32),
        ],
        name="contract",
    )(amplitudes, pieces)


def on_device(left_factor, right_factor, amplitudes, heights, owner_map, row_site):
    naux, bwidth, dpiece = right_factor.shape
    rows = left_factor.shape[0]
    formers = lax.axis_size("cd")
    place = lax.axis_index("cd").astype(jnp.int32).reshape(1)
    right = jnp.transpose(right_factor, (1, 2, 0)).reshape(bwidth * dpiece, naux)
    message = form(
        heights, place, owner_map.reshape(1, rows), row_site, left_factor, right, formers
    )
    arrived = lax.all_to_all(message, "cd", split_axis=0, concat_axis=0, tiled=True)
    coded = combine(arrived, lax.axis_size("ij"), amplitudes.shape[1], bwidth * dpiece)
    pieces = lax.all_to_all(coded, "ij", split_axis=0, concat_axis=0, tiled=True)
    partial = contract(amplitudes, pieces)
    shares = lax.all_to_all(partial, "cd", split_axis=0, concat_axis=0, tiled=True)
    return shares[:, 0, 0].sum(axis=0, keepdims=True)


def solution(mesh):
    placed = (
        P("cd", None),
        P(None, None, "ij"),
        P("ij", "cd", None),
        P("cd"),
        P("cd", None, None),
        P("cd", None),
    )
    return jax.shard_map(
        on_device, mesh=mesh, in_specs=placed, out_specs=P(("ij", "cd")), check_vma=False
    )
```

```python
import functools

import jax
import jax.numpy as jnp
from jax import lax
from jax.experimental import pallas as pl
from jax.experimental.pallas import tpu as pltpu
from jax.sharding import PartitionSpec as P

SLOTS = 16
LANES = 128
KSTEPS = 8
QBITS = 14


def form_kernel(
    heights, place, owners_hbm, sites_hbm, left_hbm, right_hbm, out,
    owners, sites, left, right, acc, dispatch, sems, small_sems,
):
    rows, naux = left.shape
    cols = right.shape[0]
    block = naux // KSTEPS
    width = cols // LANES
    depth = width * SLOTS + 2
    formers = out.shape[0] // depth
    slots = formers * SLOTS
    small = (
        pltpu.make_async_copy(owners_hbm, owners, small_sems.at[0]),
        pltpu.make_async_copy(sites_hbm, sites, small_sems.at[1]),
    )
    for copy in small:
        copy.start()
    copies = []
    for k in range(KSTEPS):
        span = slice(k * block, (k + 1) * block)
        copies.append(
            (
                pltpu.make_async_copy(left_hbm.at[:, span], left.at[:, span], sems.at[0, k]),
                pltpu.make_async_copy(right_hbm.at[:, span], right.at[:, span], sems.at[1, k]),
            )
        )
        for copy in copies[-1]:
            copy.start()
    for copy in small:
        copy.wait()
    live = lax.broadcasted_iota(jnp.int32, (1, rows), 1) < heights[0]
    owner = jnp.where(live, owners[...], -1)
    hits = lax.broadcasted_iota(jnp.int32, (formers, rows), 0) == owner
    hits_f = jnp.where(hits, 1.0, 0.0)
    upto = lax.broadcasted_iota(jnp.int32, (rows, rows), 0) <= lax.broadcasted_iota(
        jnp.int32, (rows, rows), 1
    )
    upto = jnp.where(upto, 1.0, 0.0).astype(jnp.bfloat16)
    count = jnp.dot(hits_f.astype(jnp.bfloat16), upto, preferred_element_type=jnp.float32)
    within = jnp.sum(hits_f * count, axis=0, keepdims=True).astype(jnp.int32) - 1
    target = jnp.where(live, owner * SLOTS + within, -1)
    lane = within + (place[0] % (LANES // SLOTS)) * SLOTS
    at_lane = lax.broadcasted_iota(jnp.int32, (LANES, rows), 0) == lane
    at_lane = jnp.where(at_lane, 1.0, 0.0).astype(jnp.bfloat16)
    tagged = hits_f * (sites[...] + 1).astype(jnp.float32)
    tags = lax.dot_general(
        tagged.astype(jnp.bfloat16),
        at_lane,
        (((1,), (1,)), ((), ())),
        preferred_element_type=jnp.float32,
    )
    for t in range(formers):
        tag = jnp.broadcast_to(tags[t : t + 1, :], (2, LANES))
        out[t * depth + width * SLOTS : (t + 1) * depth, :] = tag.astype(jnp.bfloat16)
    chosen = lax.broadcasted_iota(jnp.int32, (slots, rows), 0) == target
    dispatch[...] = jnp.where(chosen, 1.0, 0.0).astype(jnp.bfloat16)
    for k in range(KSTEPS):
        span = slice(k * block, (k + 1) * block)
        for copy in copies[k]:
            copy.wait()
        part = lax.dot_general(
            left[:, span],
            right[:, span],
            (((1,), (1,)), ((), ())),
            preferred_element_type=jnp.float32,
        )
        acc[...] = part if k == 0 else acc[...] + part
    panel = acc[...].astype(jnp.bfloat16)
    moved = jnp.dot(dispatch[...], panel, preferred_element_type=jnp.float32)
    moved = moved.astype(jnp.bfloat16)
    for t in range(formers):
        for part in range(width):
            at = t * depth + part * SLOTS
            piece = moved[t * SLOTS : (t + 1) * SLOTS, part * LANES : (part + 1) * LANES]
            out[at : at + SLOTS, :] = piece


def form(heights, place, owners, sites, left, right, formers):
    rows, naux = left.shape
    cols = right.shape[0]
    depth = cols // LANES * SLOTS + 2
    return pl.pallas_call(
        form_kernel,
        in_specs=[
            pl.BlockSpec(memory_space=pltpu.SMEM),
            pl.BlockSpec(memory_space=pltpu.SMEM),
            pl.BlockSpec(memory_space=pl.ANY),
            pl.BlockSpec(memory_space=pl.ANY),
            pl.BlockSpec(memory_space=pl.ANY),
            pl.BlockSpec(memory_space=pl.ANY),
        ],
        out_specs=pl.BlockSpec(memory_space=pltpu.VMEM),
        out_shape=pltpu.VMEM((formers * depth, LANES), jnp.bfloat16),
        scratch_shapes=[
            pltpu.VMEM((1, rows), jnp.int32),
            pltpu.VMEM((1, rows), jnp.int32),
            pltpu.VMEM((rows, naux), jnp.bfloat16),
            pltpu.VMEM((cols, naux), jnp.bfloat16),
            pltpu.VMEM((rows, cols), jnp.float32),
            pltpu.VMEM((formers * SLOTS, rows), jnp.bfloat16),
            pltpu.SemaphoreType.DMA((2, KSTEPS)),
            pltpu.SemaphoreType.DMA((2,)),
        ],
        name="form",
    )(heights, place, owners, sites, left, right)


def combine_kernel(arrived, out, *, formers, copies):
    depth = arrived.shape[0] // formers
    width = depth // SLOTS
    piece = out.shape[0] // copies
    tile = (piece - 2) // width
    group = LANES // SLOTS
    site = lax.broadcasted_iota(jnp.int32, (tile, LANES), 0).astype(jnp.float32) + 1.0
    pickers = []
    for g in range(formers // group):
        tag = jnp.zeros((2, LANES), jnp.float32)
        for f in range(g * group, (g + 1) * group):
            at = f * depth + width * SLOTS
            tag = tag + arrived[at : at + 2, :].astype(jnp.float32)
        pickers.append(jnp.where(tag[:1] == site, 1.0, 0.0).astype(jnp.bfloat16))
    picker = jnp.concatenate(pickers, axis=1)
    powers = []
    for part in range(width):
        rows = []
        for f in range(formers):
            at = f * depth + part * SLOTS
            rows.append(arrived[at : at + SLOTS, :])
        rows = jnp.concatenate(rows, axis=0)
        sums = jnp.dot(picker, rows, preferred_element_type=jnp.float32)
        top = jnp.maximum(jnp.max(jnp.abs(sums), axis=0, keepdims=True), 2.0**-100)
        power = jnp.ceil(jnp.log(top) * 1.4426950408889634)
        coded = jnp.round(sums * jnp.exp2(QBITS - power)).astype(jnp.int32).astype(jnp.int16)
        powers.append(power)
        for copy in range(copies):
            at = copy * piece + part * tile
            out[at : at + tile, :] = coded
    powers = jnp.concatenate(powers, axis=0).astype(jnp.int32).astype(jnp.int16)
    for copy in range(copies):
        at = copy * piece + width * tile
        out[at : at + width, :] = powers


def combine(arrived, formers, copies, tile, cols):
    width = cols // LANES
    return pl.pallas_call(
        functools.partial(combine_kernel, formers=formers, copies=copies),
        in_specs=[pl.BlockSpec(memory_space=pltpu.VMEM)],
        out_specs=pl.BlockSpec(memory_space=pltpu.VMEM),
        out_shape=pltpu.VMEM((copies * (width * tile + 2), LANES), jnp.int16),
        name="combine",
    )(pltpu.with_memory_space_constraint(arrived, pltpu.VMEM))


def contract_kernel(amplitudes, pieces, out, sums, ends, *, count):
    pairs, tile, _ = amplitudes.shape
    piece = pieces.shape[0] // count
    width = (piece - 2) // tile
    dpiece = LANES // 2
    bwidth = width * 2
    low = lax.broadcasted_iota(jnp.int32, (tile, LANES), 1) < dpiece
    for two in range(count // 2):
        span = slice(two * LANES, (two + 1) * LANES)
        both = []
        for j in (2 * two, 2 * two + 1):
            at = j * piece
            powers = pieces[at + width * tile : at + width * tile + 2, :]
            powers = jnp.exp2(powers.astype(jnp.int32).astype(jnp.float32) - QBITS)
            for half in range(width):
                whole = pieces[at + half * tile : at + (half + 1) * tile, :]
                whole = whole.astype(jnp.int32).astype(jnp.float32)
                both.append(whole * powers[half : half + 1])
        for half in range(width):
            a, b = both[half], both[width + half]
            sums[2 * half, :, span] = jnp.where(low, a, pltpu.roll(b, dpiece, 1))
            sums[2 * half + 1, :, span] = jnp.where(low, pltpu.roll(a, dpiece, 1), b)
    some = 6
    for first in range(0, pairs, some):
        totals = [[jnp.zeros((8, LANES), jnp.float32) for _ in range(bwidth)] for _ in range(some)]
        for c in range(0, tile, 8):
            for d in range(0, amplitudes.shape[2], LANES):
                s = [sums[b, c : c + 8, d : d + LANES] for b in range(bwidth)]
                for i in range(some):
                    t = amplitudes[first + i, c : c + 8, d : d + LANES]
                    for b in range(bwidth):
                        totals[i][b] = totals[i][b] + t * s[b]
        for i in range(some):
            for b in range(bwidth):
                at = (first + i) * bwidth + b
                ends[at : at + 1, :] = jnp.sum(totals[i][b], axis=0, keepdims=True)
    total = jnp.sum(ends[...], axis=1, keepdims=True)
    out[...] = jnp.broadcast_to(total, ends.shape)[:, None, :]


def contract(amplitudes, pieces, count, bwidth):
    pairs, tile, virt = amplitudes.shape
    return pl.pallas_call(
        functools.partial(contract_kernel, count=count),
        in_specs=[pl.BlockSpec(memory_space=pltpu.VMEM), pl.BlockSpec(memory_space=pltpu.VMEM)],
        out_specs=pl.BlockSpec(memory_space=pltpu.VMEM),
        out_shape=pltpu.VMEM((pairs * bwidth, 1, LANES), jnp.float32),
        scratch_shapes=[
            pltpu.VMEM((bwidth, tile, virt), jnp.float32),
            pltpu.VMEM((pairs * bwidth, LANES), jnp.float32),
        ],
        name="contract",
    )(
        pltpu.with_memory_space_constraint(amplitudes, pltpu.VMEM),
        pltpu.with_memory_space_constraint(pieces, pltpu.VMEM),
    )


def exchanged(rows, axis):
    count = lax.axis_size(axis)
    tiles = rows.reshape(count, rows.shape[0] // (2 * count), 2, LANES)
    tiles = lax.all_to_all(tiles, axis, split_axis=0, concat_axis=0, tiled=True)
    return tiles.reshape(rows.shape)


def on_device(left_factor, right_factor, amplitudes, heights, owner_map, row_site):
    naux, bwidth, dpiece = right_factor.shape
    rows = left_factor.shape[0]
    formers = lax.axis_size("cd")
    place = lax.axis_index("cd").astype(jnp.int32).reshape(1)
    right = jnp.transpose(right_factor, (1, 2, 0)).reshape(bwidth * dpiece, naux)
    message = form(
        heights, place, owner_map.reshape(1, rows), row_site, left_factor, right, formers
    )
    arrived = exchanged(message, "cd")
    parts = lax.axis_size("ij")
    coded = combine(arrived, formers, parts, amplitudes.shape[1], bwidth * dpiece)
    pieces = exchanged(coded, "ij")
    partial = contract(amplitudes, pieces, parts, bwidth)
    shares = lax.all_to_all(partial, "cd", split_axis=0, concat_axis=0, tiled=True)
    return shares[:, 0, 0].sum(axis=0, keepdims=True)


def solution(mesh):
    placed = (
        P("cd", None),
        P(None, None, "ij"),
        P("ij", "cd", None),
        P("cd"),
        P("cd", None, None),
        P("cd", None),
    )
    return jax.shard_map(
        on_device, mesh=mesh, in_specs=placed, out_specs=P(("ij", "cd")), check_vma=False
    )
```

```python
import functools

import jax
import jax.numpy as jnp
from jax import lax
from jax.experimental import pallas as pl
from jax.experimental.pallas import tpu as pltpu
from jax.sharding import PartitionSpec as P

SLOTS = 16
LANES = 128
EARLY = 3
CORES = 2
SIDE = 2
QBITS = 14


def form_kernel(
    heights, place, owners_hbm, sites_hbm, left_hbm, right_hbm, out,
    owners, sites, left, right, acc, dispatch, sems, small_sems,
):
    rows, naux = left.shape
    cols = right.shape[0]
    width = cols // LANES
    depth = width * SLOTS + 2
    formers = out.shape[0] // depth
    slots = formers * SLOTS
    small = (
        pltpu.make_async_copy(owners_hbm, owners, small_sems.at[0]),
        pltpu.make_async_copy(sites_hbm, sites, small_sems.at[1]),
    )
    for copy in small:
        copy.start()
    spans = [slice(0, naux * EARLY // 4), slice(naux * EARLY // 4, naux)]
    copies = []
    for k, span in enumerate(spans):
        copies.append(
            (
                pltpu.make_async_copy(left_hbm.at[:, span], left.at[:, span], sems.at[0, k]),
                pltpu.make_async_copy(right_hbm.at[:, span], right.at[:, span], sems.at[1, k]),
            )
        )
    for copy in copies[0]:
        copy.start()
    for copy in small:
        copy.wait()
    live = lax.broadcasted_iota(jnp.int32, (1, rows), 1) < heights[0]
    planes = formers // (CORES * SIDE)
    tile = owners[...]
    side = jnp.where(tile >= planes * CORES, 1, 0)
    inner = tile - side * planes * CORES
    plane = lax.shift_right_logical(inner, 1)
    owner = (side * CORES + (inner & 1)) * planes + plane
    owner = jnp.where(live, owner, -1)
    hits = lax.broadcasted_iota(jnp.int32, (formers, rows), 0) == owner
    hits_f = jnp.where(hits, 1.0, 0.0)
    upto = lax.broadcasted_iota(jnp.int32, (rows, rows), 0) <= lax.broadcasted_iota(
        jnp.int32, (rows, rows), 1
    )
    upto = jnp.where(upto, 1.0, 0.0).astype(jnp.bfloat16)
    count = jnp.dot(hits_f.astype(jnp.bfloat16), upto, preferred_element_type=jnp.float32)
    within = jnp.sum(hits_f * count, axis=0, keepdims=True).astype(jnp.int32) - 1
    target = jnp.where(live, owner * SLOTS + within, -1)
    mine = jnp.where(place[0] >= planes * CORES, CORES, 0) + (place[0] & 1)
    run = (mine * planes + plane) & (LANES // SLOTS - 1)
    lane = jnp.where(live, within + run * SLOTS, -1)
    at_lane = lax.broadcasted_iota(jnp.int32, (LANES, rows), 0) == lane
    at_lane = jnp.where(at_lane, 1.0, 0.0).astype(jnp.bfloat16)
    tagged = hits_f * (sites[...] + 1).astype(jnp.float32)
    tags = lax.dot_general(
        tagged.astype(jnp.bfloat16),
        at_lane,
        (((1,), (1,)), ((), ())),
        preferred_element_type=jnp.float32,
    )
    for t in range(formers):
        tag = jnp.broadcast_to(tags[t : t + 1, :], (2, LANES))
        out[t * depth + width * SLOTS : (t + 1) * depth, :] = tag.astype(jnp.bfloat16)
    chosen = lax.broadcasted_iota(jnp.int32, (slots, rows), 0) == target
    dispatch[...] = jnp.where(chosen, 1.0, 0.0).astype(jnp.bfloat16)
    for copy in copies[1]:
        copy.start()
    for k, span in enumerate(spans):
        for copy in copies[k]:
            copy.wait()
        part = lax.dot_general(
            left[:, span],
            right[:, span],
            (((1,), (1,)), ((), ())),
            preferred_element_type=jnp.float32,
        )
        acc[...] = part if k == 0 else acc[...] + part
    panel = acc[...].astype(jnp.bfloat16)
    moved = jnp.dot(dispatch[...], panel, preferred_element_type=jnp.float32)
    moved = moved.astype(jnp.bfloat16)
    for t in range(formers):
        for part in range(width):
            at = t * depth + part * SLOTS
            piece = moved[t * SLOTS : (t + 1) * SLOTS, part * LANES : (part + 1) * LANES]
            out[at : at + SLOTS, :] = piece


def form(heights, place, owners, sites, left, right, formers):
    rows, naux = left.shape
    cols = right.shape[0]
    depth = cols // LANES * SLOTS + 2
    return pl.pallas_call(
        form_kernel,
        in_specs=[
            pl.BlockSpec(memory_space=pltpu.SMEM),
            pl.BlockSpec(memory_space=pltpu.SMEM),
            pl.BlockSpec(memory_space=pl.ANY),
            pl.BlockSpec(memory_space=pl.ANY),
            pl.BlockSpec(memory_space=pl.ANY),
            pl.BlockSpec(memory_space=pl.ANY),
        ],
        out_specs=pl.BlockSpec(memory_space=pltpu.VMEM),
        out_shape=pltpu.VMEM((formers * depth, LANES), jnp.bfloat16),
        scratch_shapes=[
            pltpu.VMEM((1, rows), jnp.int32),
            pltpu.VMEM((1, rows), jnp.int32),
            pltpu.VMEM((rows, naux), jnp.bfloat16),
            pltpu.VMEM((cols, naux), jnp.bfloat16),
            pltpu.VMEM((rows, cols), jnp.float32),
            pltpu.VMEM((formers * SLOTS, rows), jnp.bfloat16),
            pltpu.SemaphoreType.DMA((2, 2)),
            pltpu.SemaphoreType.DMA((2,)),
        ],
        name="form",
    )(heights, place, owners, sites, left, right)


def encoded(sums):
    top = jnp.maximum(jnp.max(jnp.abs(sums), axis=0, keepdims=True), 2.0**-100)
    power = jnp.ceil(jnp.log(top) * 1.4426950408889634)
    return jnp.round(sums * jnp.exp2(QBITS - power)).astype(jnp.int32).astype(jnp.int16), power


def decoded(piece, at, tile, width):
    powers = piece[at + width * tile : at + width * tile + 2, :]
    powers = jnp.exp2(powers.astype(jnp.int32).astype(jnp.float32) - QBITS)
    parts = []
    for part in range(width):
        whole = piece[at + part * tile : at + (part + 1) * tile, :]
        parts.append(whole.astype(jnp.int32).astype(jnp.float32) * powers[part : part + 1])
    return parts


def collate_kernel(arrived, out, *, runs, planes):
    depth = arrived.shape[0] // runs
    width = depth // SLOTS
    piece = out.shape[0] // planes
    tile = (piece - 2) // width
    group = LANES // SLOTS
    step = 32.0
    codes = []
    for g in range(runs // group):
        tag = jnp.zeros((2, LANES), jnp.float32)
        for r in range(g * group, (g + 1) * group):
            at = r * depth + width * SLOTS
            tag = tag + arrived[at : at + 2, :].astype(jnp.float32)
        run = lax.shift_right_logical(lax.broadcasted_iota(jnp.int32, (1, LANES), 1), 4) + g * group
        plane = run
        for wrap in range(planes, runs, planes):
            plane = plane - jnp.where(run >= wrap, planes, 0)
        codes.append(jnp.where(tag[:1] > 0.0, tag[:1] + step * plane.astype(jnp.float32), 0.0))
    codes = jnp.concatenate(codes, axis=1)
    site = lax.broadcasted_iota(jnp.int32, (tile, codes.shape[1]), 0).astype(jnp.float32) + 1.0
    pickers = [jnp.where(codes == site + step * z, 1.0, 0.0) for z in range(planes)]
    picker = jnp.concatenate(pickers, axis=0).astype(jnp.bfloat16)
    rows = []
    for r in range(runs):
        parts = []
        for part in range(width):
            at = r * depth + part * SLOTS
            parts.append(arrived[at : at + SLOTS, :])
        rows.append(jnp.concatenate(parts, axis=1))
    rows = jnp.concatenate(rows, axis=0)
    sums = jnp.dot(picker, rows, preferred_element_type=jnp.float32)
    for z in range(planes):
        powers = []
        for part in range(width):
            coded, power = encoded(
                sums[z * tile : (z + 1) * tile, part * LANES : (part + 1) * LANES]
            )
            at = z * piece + part * tile
            out[at : at + tile, :] = coded
            powers.append(power)
        powers = jnp.concatenate(powers, axis=0).astype(jnp.int32).astype(jnp.int16)
        at = z * piece + width * tile
        out[at : at + width, :] = powers


def collate(arrived, runs, planes, tile, cols):
    return pl.pallas_call(
        functools.partial(collate_kernel, runs=runs, planes=planes),
        in_specs=[pl.BlockSpec(memory_space=pltpu.VMEM)],
        out_specs=pl.BlockSpec(memory_space=pltpu.VMEM),
        out_shape=pltpu.VMEM((planes * (cols // LANES * tile + 2), LANES), jnp.int16),
        name="collate",
    )(pltpu.with_memory_space_constraint(arrived, pltpu.VMEM))


def combine_kernel(arrived, out, *, planes, copies, tile, width):
    piece = width * tile + 2
    totals = decoded(arrived, 0, tile, width)
    for z in range(1, planes):
        parts = decoded(arrived, z * piece, tile, width)
        totals = [total + part for total, part in zip(totals, parts)]
    powers = []
    for part in range(width):
        coded, power = encoded(totals[part])
        powers.append(power)
        for copy in range(copies):
            at = copy * piece + part * tile
            out[at : at + tile, :] = coded
    powers = jnp.concatenate(powers, axis=0).astype(jnp.int32).astype(jnp.int16)
    for copy in range(copies):
        at = copy * piece + width * tile
        out[at : at + width, :] = powers


def combine(arrived, planes, copies, tile, cols):
    width = cols // LANES
    return pl.pallas_call(
        functools.partial(combine_kernel, planes=planes, copies=copies, tile=tile, width=width),
        in_specs=[pl.BlockSpec(memory_space=pltpu.VMEM)],
        out_specs=pl.BlockSpec(memory_space=pltpu.VMEM),
        out_shape=pltpu.VMEM((copies * (width * tile + 2), LANES), jnp.int16),
        name="combine",
    )(pltpu.with_memory_space_constraint(arrived, pltpu.VMEM))


def contract_kernel(amplitudes, pieces, out, sums, ends, *, count):
    pairs, tile, _ = amplitudes.shape
    piece = pieces.shape[0] // count
    width = (piece - 2) // tile
    dpiece = LANES // 2
    bwidth = width * 2
    low = lax.broadcasted_iota(jnp.int32, (tile, LANES), 1) < dpiece
    for two in range(count // 2):
        span = slice(two * LANES, (two + 1) * LANES)
        both = []
        for j in (2 * two, 2 * two + 1):
            both += decoded(pieces, j * piece, tile, width)
        for half in range(width):
            a, b = both[half], both[width + half]
            sums[2 * half, :, span] = jnp.where(low, a, pltpu.roll(b, dpiece, 1))
            sums[2 * half + 1, :, span] = jnp.where(low, pltpu.roll(a, dpiece, 1), b)
    some = 6
    for first in range(0, pairs, some):
        totals = [[jnp.zeros((8, LANES), jnp.float32) for _ in range(bwidth)] for _ in range(some)]
        for c in range(0, tile, 8):
            for d in range(0, amplitudes.shape[2], LANES):
                s = [sums[b, c : c + 8, d : d + LANES] for b in range(bwidth)]
                for i in range(some):
                    t = amplitudes[first + i, c : c + 8, d : d + LANES]
                    for b in range(bwidth):
                        totals[i][b] = totals[i][b] + t * s[b]
        for i in range(some):
            for b in range(bwidth):
                at = (first + i) * bwidth + b
                ends[at : at + 1, :] = jnp.sum(totals[i][b], axis=0, keepdims=True)
    total = jnp.sum(ends[...], axis=1, keepdims=True)
    out[...] = jnp.broadcast_to(total, ends.shape)[:, None, :]


def contract(amplitudes, pieces, count, bwidth):
    pairs, tile, virt = amplitudes.shape
    return pl.pallas_call(
        functools.partial(contract_kernel, count=count),
        in_specs=[pl.BlockSpec(memory_space=pltpu.VMEM), pl.BlockSpec(memory_space=pltpu.VMEM)],
        out_specs=pl.BlockSpec(memory_space=pltpu.VMEM),
        out_shape=pltpu.VMEM((pairs * bwidth, 1, LANES), jnp.float32),
        scratch_shapes=[
            pltpu.VMEM((bwidth, tile, virt), jnp.float32),
            pltpu.VMEM((pairs * bwidth, LANES), jnp.float32),
        ],
        name="contract",
    )(
        pltpu.with_memory_space_constraint(amplitudes, pltpu.VMEM),
        pltpu.with_memory_space_constraint(pieces, pltpu.VMEM),
    )


def exchanged(rows, axis, groups=None):
    count = len(groups[0]) if groups else lax.axis_size(axis)
    tiles = rows.reshape(count, rows.shape[0] // (2 * count), 2, LANES)
    tiles = lax.all_to_all(
        tiles, axis, split_axis=0, concat_axis=0, tiled=True, axis_index_groups=groups
    )
    return tiles.reshape(rows.shape)


def on_device(left_factor, right_factor, amplitudes, heights, owner_map, row_site):
    naux, bwidth, dpiece = right_factor.shape
    cols = bwidth * dpiece
    rows = left_factor.shape[0]
    tile = amplitudes.shape[1]
    formers = lax.axis_size("cd")
    parts = lax.axis_size("ij")
    planes = formers // (CORES * SIDE)
    at = [
        [[(s * planes + z) * CORES + c for c in range(CORES)] for z in range(planes)]
        for s in range(SIDE)
    ]
    beside = [[at[s][z][c] for s in range(SIDE) for c in range(CORES)] for z in range(planes)]
    along = [[at[s][z][c] for z in range(planes)] for s in range(SIDE) for c in range(CORES)]
    place = lax.axis_index("cd").astype(jnp.int32).reshape(1)
    right = jnp.transpose(right_factor, (1, 2, 0)).reshape(cols, naux)
    message = form(
        heights, place, owner_map.reshape(1, rows), row_site, left_factor, right, formers
    )
    arrived = exchanged(message, "cd", beside)
    collated = collate(arrived, formers, planes, tile, cols)
    planar = exchanged(collated, "cd", along)
    coded = combine(planar, planes, parts, tile, cols)
    pieces = exchanged(coded, "ij")
    partial = contract(amplitudes, pieces, parts, bwidth)
    shares = lax.all_to_all(partial, "cd", split_axis=0, concat_axis=0, tiled=True)
    return shares[:, 0, 0].sum(axis=0, keepdims=True)


def solution(mesh):
    placed = (
        P("cd", None),
        P(None, None, "ij"),
        P("ij", "cd", None),
        P("cd"),
        P("cd", None, None),
        P("cd", None),
    )
    return jax.shard_map(
        on_device, mesh=mesh, in_specs=placed, out_specs=P(("ij", "cd")), check_vma=False
    )
```

```python
import functools

import jax
import jax.numpy as jnp
from jax import lax
from jax.experimental import pallas as pl
from jax.experimental.pallas import tpu as pltpu
from jax.sharding import PartitionSpec as P

SLOTS = 16
LANES = 128
EARLY = 3
CORES = 2
SIDE = 2
PLANE_TURN = 9
PART_STEP = 5
PART_TURN = 4
LAST_TURN = 16
QBITS = 14


def plane_order(planes):
    half = planes // 2
    return [(at + PLANE_TURN) % planes for step in range(half) for at in (step, step + half)]


def part_order(pairs):
    return [(PART_STEP * step + PART_TURN) % pairs for step in range(pairs)]


def last_order(formers):
    return [(at + LAST_TURN) % formers for at in range(formers)]


def form_kernel(
    heights, place, owners_hbm, sites_hbm, left_hbm, right_hbm, out,
    owners, sites, left, right, acc, dispatch, sems, small_sems,
):
    rows, naux = left.shape
    cols = right.shape[0]
    width = cols // LANES
    beside = CORES * SIDE
    depth = out.shape[0] // beside
    planes = (depth - SLOTS) // (width * SLOTS)
    formers = planes * beside
    slots = formers * SLOTS
    small = (
        pltpu.make_async_copy(owners_hbm, owners, small_sems.at[0]),
        pltpu.make_async_copy(sites_hbm, sites, small_sems.at[1]),
    )
    for copy in small:
        copy.start()
    spans = [slice(0, naux * EARLY // 4), slice(naux * EARLY // 4, naux)]
    copies = []
    for k, span in enumerate(spans):
        copies.append(
            (
                pltpu.make_async_copy(left_hbm.at[:, span], left.at[:, span], sems.at[0, k]),
                pltpu.make_async_copy(right_hbm.at[:, span], right.at[:, span], sems.at[1, k]),
            )
        )
    for copy in copies[0]:
        copy.start()
    for copy in small:
        copy.wait()
    live = lax.broadcasted_iota(jnp.int32, (1, rows), 1) < heights[0]
    tile = owners[...]
    side = jnp.where(tile >= planes * CORES, 1, 0)
    inner = tile - side * planes * CORES
    plane = lax.shift_right_logical(inner, 1)
    peer = side * CORES + (inner & 1)
    owner = jnp.where(live, peer * planes + plane, -1)
    hits = lax.broadcasted_iota(jnp.int32, (formers, rows), 0) == owner
    hits_f = jnp.where(hits, 1.0, 0.0)
    upto = lax.broadcasted_iota(jnp.int32, (rows, rows), 0) <= lax.broadcasted_iota(
        jnp.int32, (rows, rows), 1
    )
    upto = jnp.where(upto, 1.0, 0.0).astype(jnp.bfloat16)
    count = jnp.dot(hits_f.astype(jnp.bfloat16), upto, preferred_element_type=jnp.float32)
    within = jnp.sum(hits_f * count, axis=0, keepdims=True).astype(jnp.int32) - 1
    target = jnp.where(live, owner * SLOTS + within, -1)
    mine = jnp.where(place[0] >= planes * CORES, CORES, 0) + (place[0] & 1)
    run = ((mine * planes) & (LANES // SLOTS - 1)) + plane
    lane = jnp.where(live, within + (run & (LANES // SLOTS - 1)) * SLOTS, -1)
    at_lane = lax.broadcasted_iota(jnp.int32, (LANES, rows), 0) == lane
    at_lane = jnp.where(at_lane, 1.0, 0.0).astype(jnp.bfloat16)
    line = peer * SLOTS + lax.shift_right_logical(run, 3)
    at_line = lax.broadcasted_iota(jnp.int32, (beside * SLOTS, rows), 0) == line
    tagged = jnp.where(at_line, (sites[...] + 1).astype(jnp.float32), 0.0)
    tags = lax.dot_general(
        tagged.astype(jnp.bfloat16),
        at_lane,
        (((1,), (1,)), ((), ())),
        preferred_element_type=jnp.float32,
    ).astype(jnp.bfloat16)
    for q in range(beside):
        out[(q + 1) * depth - SLOTS : (q + 1) * depth, :] = tags[q * SLOTS : (q + 1) * SLOTS]
    chosen = lax.broadcasted_iota(jnp.int32, (slots, rows), 0) == target
    dispatch[...] = jnp.where(chosen, 1.0, 0.0).astype(jnp.bfloat16)
    for copy in copies[1]:
        copy.start()
    for k, span in enumerate(spans):
        for copy in copies[k]:
            copy.wait()
        part = lax.dot_general(
            left[:, span],
            right[:, span],
            (((1,), (1,)), ((), ())),
            preferred_element_type=jnp.float32,
        )
        acc[...] = part if k == 0 else acc[...] + part
    panel = acc[...].astype(jnp.bfloat16)
    moved = jnp.dot(dispatch[...], panel, preferred_element_type=jnp.float32)
    moved = moved.astype(jnp.bfloat16)
    for t in range(formers):
        for part in range(width):
            at = t // planes * depth + (t % planes * width + part) * SLOTS
            piece = moved[t * SLOTS : (t + 1) * SLOTS, part * LANES : (part + 1) * LANES]
            out[at : at + SLOTS, :] = piece


def form(heights, place, owners, sites, left, right, formers):
    rows, naux = left.shape
    cols = right.shape[0]
    size = (cols // LANES * formers + CORES * SIDE) * SLOTS
    return pl.pallas_call(
        form_kernel,
        in_specs=[
            pl.BlockSpec(memory_space=pltpu.SMEM),
            pl.BlockSpec(memory_space=pltpu.SMEM),
            pl.BlockSpec(memory_space=pl.ANY),
            pl.BlockSpec(memory_space=pl.ANY),
            pl.BlockSpec(memory_space=pl.ANY),
            pl.BlockSpec(memory_space=pl.ANY),
        ],
        out_specs=pl.BlockSpec(memory_space=pltpu.VMEM),
        out_shape=pltpu.VMEM((size, LANES), jnp.bfloat16),
        scratch_shapes=[
            pltpu.VMEM((1, rows), jnp.int32),
            pltpu.VMEM((1, rows), jnp.int32),
            pltpu.VMEM((rows, naux), jnp.bfloat16),
            pltpu.VMEM((cols, naux), jnp.bfloat16),
            pltpu.VMEM((rows, cols), jnp.float32),
            pltpu.VMEM((formers * SLOTS, rows), jnp.bfloat16),
            pltpu.SemaphoreType.DMA((2, 2)),
            pltpu.SemaphoreType.DMA((2,)),
        ],
        name="form",
    )(heights, place, owners, sites, left, right)


def encoded(sums):
    top = jnp.maximum(jnp.max(jnp.abs(sums), axis=0, keepdims=True), 2.0**-100)
    power = jnp.ceil(jnp.log(top) * 1.4426950408889634)
    return jnp.round(sums * jnp.exp2(QBITS - power)).astype(jnp.int32).astype(jnp.int16), power


def decoded(piece, at, tile, width):
    powers = piece[at + width * tile : at + width * tile + 2, :]
    powers = jnp.exp2(powers.astype(jnp.int32).astype(jnp.float32) - QBITS)
    parts = []
    for part in range(width):
        whole = piece[at + part * tile : at + (part + 1) * tile, :]
        parts.append(whole.astype(jnp.int32).astype(jnp.float32) * powers[part : part + 1])
    return parts


def collate_kernel(arrived, out, *, planes, width):
    beside = CORES * SIDE
    depth = arrived.shape[0] // beside
    runs = planes * beside
    piece = out.shape[0] // planes
    tile = (piece - 2) // width
    group = LANES // SLOTS
    step = 32.0
    tags = [jnp.zeros((1, LANES), jnp.float32) for _ in range(runs // group)]
    for q in range(beside):
        lines = arrived[(q + 1) * depth - SLOTS : (q + 1) * depth, :].astype(jnp.float32)
        first = q * planes // group
        for g in range(first, ((q + 1) * planes - 1) // group + 1):
            tags[g] = tags[g] + lines[g - first : g - first + 1]
    codes = []
    for g in range(runs // group):
        run = lax.shift_right_logical(lax.broadcasted_iota(jnp.int32, (1, LANES), 1), 4) + g * group
        plane = run
        for wrap in range(planes, runs, planes):
            plane = plane - jnp.where(run >= wrap, planes, 0)
        codes.append(jnp.where(tags[g] > 0.0, tags[g] + step * plane.astype(jnp.float32), 0.0))
    codes = jnp.concatenate(codes, axis=1)
    site = lax.broadcasted_iota(jnp.int32, (tile, codes.shape[1]), 0).astype(jnp.float32) + 1.0
    pickers = [jnp.where(codes == site + step * z, 1.0, 0.0) for z in range(planes)]
    picker = jnp.concatenate(pickers, axis=0).astype(jnp.bfloat16)
    rows = []
    for r in range(runs):
        parts = []
        for part in range(width):
            at = r // planes * depth + (r % planes * width + part) * SLOTS
            parts.append(arrived[at : at + SLOTS, :])
        rows.append(jnp.concatenate(parts, axis=1))
    rows = jnp.concatenate(rows, axis=0)
    sums = jnp.dot(picker, rows, preferred_element_type=jnp.float32)
    order = plane_order(planes)
    for z in range(planes):
        powers = []
        first = order.index(z) * piece
        for part in range(width):
            coded, power = encoded(
                sums[z * tile : (z + 1) * tile, part * LANES : (part + 1) * LANES]
            )
            at = first + part * tile
            out[at : at + tile, :] = coded
            powers.append(power)
        powers = jnp.concatenate(powers, axis=0).astype(jnp.int32).astype(jnp.int16)
        at = first + width * tile
        out[at : at + width, :] = powers


def collate(arrived, planes, tile, cols):
    return pl.pallas_call(
        functools.partial(collate_kernel, planes=planes, width=cols // LANES),
        in_specs=[pl.BlockSpec(memory_space=pltpu.VMEM)],
        out_specs=pl.BlockSpec(memory_space=pltpu.VMEM),
        out_shape=pltpu.VMEM((planes * (cols // LANES * tile + 2), LANES), jnp.int16),
        name="collate",
    )(pltpu.with_memory_space_constraint(arrived, pltpu.VMEM))


def combine_kernel(arrived, out, *, planes, copies, tile, width):
    piece = width * tile + 2
    totals = decoded(arrived, 0, tile, width)
    for z in range(1, planes):
        parts = decoded(arrived, z * piece, tile, width)
        totals = [total + part for total, part in zip(totals, parts)]
    powers = []
    for part in range(width):
        coded, power = encoded(totals[part])
        powers.append(power)
        for copy in range(copies):
            at = copy * piece + part * tile
            out[at : at + tile, :] = coded
    powers = jnp.concatenate(powers, axis=0).astype(jnp.int32).astype(jnp.int16)
    for copy in range(copies):
        at = copy * piece + width * tile
        out[at : at + width, :] = powers


def combine(arrived, planes, copies, tile, cols):
    width = cols // LANES
    return pl.pallas_call(
        functools.partial(combine_kernel, planes=planes, copies=copies, tile=tile, width=width),
        in_specs=[pl.BlockSpec(memory_space=pltpu.VMEM)],
        out_specs=pl.BlockSpec(memory_space=pltpu.VMEM),
        out_shape=pltpu.VMEM((copies * (width * tile + 2), LANES), jnp.int16),
        name="combine",
    )(pltpu.with_memory_space_constraint(arrived, pltpu.VMEM))


def contract_kernel(amplitudes, pieces, out, sums, ends, *, count):
    pairs, tile, _ = amplitudes.shape
    piece = pieces.shape[0] // count
    width = (piece - 2) // tile
    dpiece = LANES // 2
    bwidth = width * 2
    low = lax.broadcasted_iota(jnp.int32, (tile, LANES), 1) < dpiece
    for two, place in enumerate(part_order(count // 2)):
        span = slice(place * LANES, (place + 1) * LANES)
        both = []
        for j in (2 * two, 2 * two + 1):
            both += decoded(pieces, j * piece, tile, width)
        for half in range(width):
            a, b = both[half], both[width + half]
            sums[2 * half, :, span] = jnp.where(low, a, pltpu.roll(b, dpiece, 1))
            sums[2 * half + 1, :, span] = jnp.where(low, pltpu.roll(a, dpiece, 1), b)
    order = last_order(pairs * bwidth)
    some = 6
    for first in range(0, pairs, some):
        totals = [[jnp.zeros((8, LANES), jnp.float32) for _ in range(bwidth)] for _ in range(some)]
        for c in range(0, tile, 8):
            for d in range(0, amplitudes.shape[2], LANES):
                s = [sums[b, c : c + 8, d : d + LANES] for b in range(bwidth)]
                for i in range(some):
                    t = amplitudes[first + i, c : c + 8, d : d + LANES]
                    for b in range(bwidth):
                        totals[i][b] = totals[i][b] + t * s[b]
        for i in range(some):
            for b in range(bwidth):
                at = order.index((first + i) * bwidth + b)
                ends[at : at + 1, :] = jnp.sum(totals[i][b], axis=0, keepdims=True)
    total = jnp.sum(ends[...], axis=1, keepdims=True)
    out[...] = jnp.broadcast_to(total, ends.shape)[:, None, :]


def contract(amplitudes, pieces, count, bwidth):
    pairs, tile, virt = amplitudes.shape
    return pl.pallas_call(
        functools.partial(contract_kernel, count=count),
        in_specs=[pl.BlockSpec(memory_space=pltpu.VMEM), pl.BlockSpec(memory_space=pltpu.VMEM)],
        out_specs=pl.BlockSpec(memory_space=pltpu.VMEM),
        out_shape=pltpu.VMEM((pairs * bwidth, 1, LANES), jnp.float32),
        scratch_shapes=[
            pltpu.VMEM((bwidth, tile, virt), jnp.float32),
            pltpu.VMEM((pairs * bwidth, LANES), jnp.float32),
        ],
        name="contract",
    )(
        pltpu.with_memory_space_constraint(amplitudes, pltpu.VMEM),
        pltpu.with_memory_space_constraint(pieces, pltpu.VMEM),
    )


def finish_kernel(shares, out):
    out[...] = jnp.sum(shares[:, 0, :], axis=0, keepdims=True)


def finish(shares):
    return pl.pallas_call(
        finish_kernel,
        in_specs=[pl.BlockSpec(memory_space=pltpu.VMEM)],
        out_specs=pl.BlockSpec(memory_space=pltpu.VMEM),
        out_shape=pltpu.VMEM((1, shares.shape[2]), jnp.float32),
        name="finish",
    )(pltpu.with_memory_space_constraint(shares, pltpu.VMEM))


def exchanged(rows, axis, groups=None):
    count = len(groups[0]) if groups else lax.axis_size(axis)
    tiles = rows.reshape(count, rows.shape[0] // (2 * count), 2, LANES)
    tiles = lax.all_to_all(
        tiles, axis, split_axis=0, concat_axis=0, tiled=True, axis_index_groups=groups
    )
    return tiles.reshape(rows.shape)


def on_device(left_factor, right_factor, amplitudes, heights, owner_map, row_site):
    naux, bwidth, dpiece = right_factor.shape
    cols = bwidth * dpiece
    rows = left_factor.shape[0]
    tile = amplitudes.shape[1]
    formers = lax.axis_size("cd")
    parts = lax.axis_size("ij")
    planes = formers // (CORES * SIDE)
    at = [
        [[(s * planes + z) * CORES + c for c in range(CORES)] for z in range(planes)]
        for s in range(SIDE)
    ]
    beside = [[at[s][z][c] for s in range(SIDE) for c in range(CORES)] for z in range(planes)]
    order = plane_order(planes)
    along = [[at[s][z][c] for z in order] for s in range(SIDE) for c in range(CORES)]
    across = [[2 * pair + half for pair in part_order(parts // 2) for half in range(2)]]
    place = lax.axis_index("cd").astype(jnp.int32).reshape(1)
    right = jnp.transpose(right_factor, (1, 2, 0)).reshape(cols, naux)
    message = form(
        heights, place, owner_map.reshape(1, rows), row_site, left_factor, right, formers
    )
    arrived = exchanged(message, "cd", beside)
    collated = collate(arrived, planes, tile, cols)
    planar = exchanged(collated, "cd", along)
    coded = combine(planar, planes, parts, tile, cols)
    pieces = exchanged(coded, "ij", across)
    partial = contract(amplitudes, pieces, parts, bwidth)
    shares = lax.all_to_all(
        partial,
        "cd",
        split_axis=0,
        concat_axis=0,
        tiled=True,
        axis_index_groups=[last_order(formers)],
    )
    return finish(shares)[0, :1]


def solution(mesh):
    placed = (
        P("cd", None),
        P(None, None, "ij"),
        P("ij", "cd", None),
        P("cd"),
        P("cd", None, None),
        P("cd", None),
    )
    return jax.shard_map(
        on_device, mesh=mesh, in_specs=placed, out_specs=P(("ij", "cd")), check_vma=False
    )
```

```python
import functools

import jax
import jax.numpy as jnp
from jax import lax
from jax.experimental import pallas as pl
from jax.experimental.pallas import tpu as pltpu
from jax.sharding import PartitionSpec as P

SLOTS = 16
LANES = 128
EARLY = 3
CORES = 2
SIDE = 2
PLANE_TURN = 9
PART_STEP = 5
PART_TURN = 4
LAST_TURN = 16
QBITS = 14


def plane_order(planes):
    half = planes // 2
    return [(at + PLANE_TURN) % planes for step in range(half) for at in (step, step + half)]


def part_order(pairs):
    return [(PART_STEP * step + PART_TURN) % pairs for step in range(pairs)]


def last_order(formers):
    return [(at + LAST_TURN) % formers for at in range(formers)]


def form_kernel(
    heights, place, owners_hbm, sites_hbm, left_hbm, right_hbm, out,
    owners, sites, left, right, acc, dispatch, sems, small_sems,
):
    rows, naux = left.shape
    cols = right.shape[0]
    width = cols // LANES
    beside = CORES * SIDE
    depth = out.shape[0] // beside
    planes = (depth - SLOTS) // (width * SLOTS)
    formers = planes * beside
    slots = formers * SLOTS
    small = (
        pltpu.make_async_copy(owners_hbm, owners, small_sems.at[0]),
        pltpu.make_async_copy(sites_hbm, sites, small_sems.at[1]),
    )
    for copy in small:
        copy.start()
    spans = [slice(0, naux * EARLY // 4), slice(naux * EARLY // 4, naux)]
    copies = []
    for k, span in enumerate(spans):
        copies.append(
            (
                pltpu.make_async_copy(left_hbm.at[:, span], left.at[:, span], sems.at[0, k]),
                pltpu.make_async_copy(right_hbm.at[:, span], right.at[:, span], sems.at[1, k]),
            )
        )
    for copy in copies[0]:
        copy.start()
    for copy in small:
        copy.wait()
    live = lax.broadcasted_iota(jnp.int32, (1, rows), 1) < heights[0]
    tile = owners[...]
    side = jnp.where(tile >= planes * CORES, 1, 0)
    inner = tile - side * planes * CORES
    plane = lax.shift_right_logical(inner, 1)
    peer = side * CORES + (inner & 1)
    owner = jnp.where(live, peer * planes + plane, -1)
    hits = lax.broadcasted_iota(jnp.int32, (formers, rows), 0) == owner
    hits_f = jnp.where(hits, 1.0, 0.0)
    upto = lax.broadcasted_iota(jnp.int32, (rows, rows), 0) <= lax.broadcasted_iota(
        jnp.int32, (rows, rows), 1
    )
    upto = jnp.where(upto, 1.0, 0.0).astype(jnp.bfloat16)
    count = jnp.dot(hits_f.astype(jnp.bfloat16), upto, preferred_element_type=jnp.float32)
    within = jnp.sum(hits_f * count, axis=0, keepdims=True).astype(jnp.int32) - 1
    target = jnp.where(live, owner * SLOTS + within, -1)
    mine = jnp.where(place[0] >= planes * CORES, CORES, 0) + (place[0] & 1)
    run = ((mine * planes) & (LANES // SLOTS - 1)) + plane
    lane = jnp.where(live, within + (run & (LANES // SLOTS - 1)) * SLOTS, -1)
    at_lane = lax.broadcasted_iota(jnp.int32, (LANES, rows), 0) == lane
    at_lane = jnp.where(at_lane, 1.0, 0.0).astype(jnp.bfloat16)
    line = peer * SLOTS + lax.shift_right_logical(run, 3)
    at_line = lax.broadcasted_iota(jnp.int32, (beside * SLOTS, rows), 0) == line
    tagged = jnp.where(at_line, (sites[...] + 1).astype(jnp.float32), 0.0)
    tags = lax.dot_general(
        tagged.astype(jnp.bfloat16),
        at_lane,
        (((1,), (1,)), ((), ())),
        preferred_element_type=jnp.float32,
    ).astype(jnp.bfloat16)
    for q in range(beside):
        out[(q + 1) * depth - SLOTS : (q + 1) * depth, :] = tags[q * SLOTS : (q + 1) * SLOTS]
    chosen = lax.broadcasted_iota(jnp.int32, (slots, rows), 0) == target
    dispatch[...] = jnp.where(chosen, 1.0, 0.0).astype(jnp.bfloat16)
    for copy in copies[1]:
        copy.start()
    for k, span in enumerate(spans):
        for copy in copies[k]:
            copy.wait()
        part = lax.dot_general(
            left[:, span],
            right[:, span],
            (((1,), (1,)), ((), ())),
            preferred_element_type=jnp.float32,
        )
        acc[...] = part if k == 0 else acc[...] + part
    panel = acc[...].astype(jnp.bfloat16)
    moved = jnp.dot(dispatch[...], panel, preferred_element_type=jnp.float32)
    moved = moved.astype(jnp.bfloat16)
    for t in range(formers):
        for part in range(width):
            at = t // planes * depth + (t % planes * width + part) * SLOTS
            piece = moved[t * SLOTS : (t + 1) * SLOTS, part * LANES : (part + 1) * LANES]
            out[at : at + SLOTS, :] = piece


def form(heights, place, owners, sites, left, right, formers):
    rows, naux = left.shape
    cols = right.shape[0]
    size = (cols // LANES * formers + CORES * SIDE) * SLOTS
    return pl.pallas_call(
        form_kernel,
        in_specs=[
            pl.BlockSpec(memory_space=pltpu.SMEM),
            pl.BlockSpec(memory_space=pltpu.SMEM),
            pl.BlockSpec(memory_space=pl.ANY),
            pl.BlockSpec(memory_space=pl.ANY),
            pl.BlockSpec(memory_space=pl.ANY),
            pl.BlockSpec(memory_space=pl.ANY),
        ],
        out_specs=pl.BlockSpec(memory_space=pltpu.VMEM),
        out_shape=pltpu.VMEM((size, LANES), jnp.bfloat16),
        scratch_shapes=[
            pltpu.VMEM((1, rows), jnp.int32),
            pltpu.VMEM((1, rows), jnp.int32),
            pltpu.VMEM((rows, naux), jnp.bfloat16),
            pltpu.VMEM((cols, naux), jnp.bfloat16),
            pltpu.VMEM((rows, cols), jnp.float32),
            pltpu.VMEM((formers * SLOTS, rows), jnp.bfloat16),
            pltpu.SemaphoreType.DMA((2, 2)),
            pltpu.SemaphoreType.DMA((2,)),
        ],
        name="form",
    )(heights, place, owners, sites, left, right)


def encoded(sums):
    top = jnp.maximum(jnp.max(jnp.abs(sums), axis=0, keepdims=True), 2.0**-100)
    power = jnp.ceil(jnp.log(top) * 1.4426950408889634)
    return jnp.round(sums * jnp.exp2(QBITS - power)).astype(jnp.int32).astype(jnp.int16), power


def decoded(piece, at, tile, width):
    powers = piece[at + width * tile : at + width * tile + 2, :]
    powers = jnp.exp2(powers.astype(jnp.int32).astype(jnp.float32) - QBITS)
    parts = []
    for part in range(width):
        whole = piece[at + part * tile : at + (part + 1) * tile, :]
        parts.append(whole.astype(jnp.int32).astype(jnp.float32) * powers[part : part + 1])
    return parts


def collate_kernel(arrived, out, *, planes, width):
    beside = CORES * SIDE
    depth = arrived.shape[0] // beside
    runs = planes * beside
    piece = out.shape[0] // planes
    tile = (piece - 2) // width
    group = LANES // SLOTS
    step = 32.0
    tags = [jnp.zeros((1, LANES), jnp.float32) for _ in range(runs // group)]
    for q in range(beside):
        lines = arrived[(q + 1) * depth - SLOTS : (q + 1) * depth, :].astype(jnp.float32)
        first = q * planes // group
        for g in range(first, ((q + 1) * planes - 1) // group + 1):
            tags[g] = tags[g] + lines[g - first : g - first + 1]
    codes = []
    for g in range(runs // group):
        run = lax.shift_right_logical(lax.broadcasted_iota(jnp.int32, (1, LANES), 1), 4) + g * group
        plane = run
        for wrap in range(planes, runs, planes):
            plane = plane - jnp.where(run >= wrap, planes, 0)
        codes.append(jnp.where(tags[g] > 0.0, tags[g] + step * plane.astype(jnp.float32), 0.0))
    codes = jnp.concatenate(codes, axis=1)
    site = lax.broadcasted_iota(jnp.int32, (tile, codes.shape[1]), 0).astype(jnp.float32) + 1.0
    pickers = [jnp.where(codes == site + step * z, 1.0, 0.0) for z in range(planes)]
    picker = jnp.concatenate(pickers, axis=0).astype(jnp.bfloat16)
    rows = []
    for r in range(runs):
        parts = []
        for part in range(width):
            at = r // planes * depth + (r % planes * width + part) * SLOTS
            parts.append(arrived[at : at + SLOTS, :])
        rows.append(jnp.concatenate(parts, axis=1))
    rows = jnp.concatenate(rows, axis=0)
    sums = jnp.dot(picker, rows, preferred_element_type=jnp.float32)
    order = plane_order(planes)
    for z in range(planes):
        powers = []
        first = order.index(z) * piece
        for part in range(width):
            coded, power = encoded(
                sums[z * tile : (z + 1) * tile, part * LANES : (part + 1) * LANES]
            )
            at = first + part * tile
            out[at : at + tile, :] = coded
            powers.append(power)
        powers = jnp.concatenate(powers, axis=0).astype(jnp.int32).astype(jnp.int16)
        at = first + width * tile
        out[at : at + width, :] = powers


def collate(arrived, planes, tile, cols):
    return pl.pallas_call(
        functools.partial(collate_kernel, planes=planes, width=cols // LANES),
        in_specs=[pl.BlockSpec(memory_space=pltpu.VMEM)],
        out_specs=pl.BlockSpec(memory_space=pltpu.VMEM),
        out_shape=pltpu.VMEM((planes * (cols // LANES * tile + 2), LANES), jnp.int16),
        name="collate",
    )(pltpu.with_memory_space_constraint(arrived, pltpu.VMEM))


def combine_kernel(arrived, out, *, planes, copies, tile, width):
    piece = width * tile + 2
    totals = decoded(arrived, 0, tile, width)
    for z in range(1, planes):
        parts = decoded(arrived, z * piece, tile, width)
        totals = [total + part for total, part in zip(totals, parts)]
    powers = []
    for part in range(width):
        coded, power = encoded(totals[part])
        powers.append(power)
        for copy in range(copies):
            at = copy * piece + part * tile
            out[at : at + tile, :] = coded
    powers = jnp.concatenate(powers, axis=0).astype(jnp.int32).astype(jnp.int16)
    for copy in range(copies):
        at = copy * piece + width * tile
        out[at : at + width, :] = powers


def combine(arrived, planes, copies, tile, cols):
    width = cols // LANES
    return pl.pallas_call(
        functools.partial(combine_kernel, planes=planes, copies=copies, tile=tile, width=width),
        in_specs=[pl.BlockSpec(memory_space=pltpu.VMEM)],
        out_specs=pl.BlockSpec(memory_space=pltpu.VMEM),
        out_shape=pltpu.VMEM((copies * (width * tile + 2), LANES), jnp.int16),
        name="combine",
    )(pltpu.with_memory_space_constraint(arrived, pltpu.VMEM))


def contract_kernel(amplitudes, pieces, out, sums, ends, *, count):
    pairs, tile, _ = amplitudes.shape
    piece = pieces.shape[0] // count
    width = (piece - 2) // tile
    dpiece = LANES // 2
    bwidth = width * 2
    low = lax.broadcasted_iota(jnp.int32, (tile, LANES), 1) < dpiece
    for two, place in enumerate(part_order(count // 2)):
        span = slice(place * LANES, (place + 1) * LANES)
        both = []
        for j in (2 * two + 1, 2 * two):
            both += decoded(pieces, j * piece, tile, width)
        for half in range(width):
            a, b = both[half], both[width + half]
            sums[2 * half, :, span] = jnp.where(low, a, pltpu.roll(b, dpiece, 1))
            sums[2 * half + 1, :, span] = jnp.where(low, pltpu.roll(a, dpiece, 1), b)
    order = last_order(pairs * bwidth)
    some = 6
    for first in range(0, pairs, some):
        totals = [[jnp.zeros((8, LANES), jnp.float32) for _ in range(bwidth)] for _ in range(some)]
        for c in range(0, tile, 8):
            for d in range(0, amplitudes.shape[2], LANES):
                s = [sums[b, c : c + 8, d : d + LANES] for b in range(bwidth)]
                for i in range(some):
                    t = amplitudes[first + i, c : c + 8, d : d + LANES]
                    for b in range(bwidth):
                        totals[i][b] = totals[i][b] + t * s[b]
        for i in range(some):
            for b in range(bwidth):
                at = order.index((first + i) * bwidth + b)
                ends[at : at + 1, :] = jnp.sum(totals[i][b], axis=0, keepdims=True)
    total = jnp.sum(ends[...], axis=1, keepdims=True)
    out[...] = jnp.broadcast_to(total, ends.shape)[:, None, :]


def contract(amplitudes, pieces, count, bwidth):
    pairs, tile, virt = amplitudes.shape
    return pl.pallas_call(
        functools.partial(contract_kernel, count=count),
        in_specs=[pl.BlockSpec(memory_space=pltpu.VMEM), pl.BlockSpec(memory_space=pltpu.VMEM)],
        out_specs=pl.BlockSpec(memory_space=pltpu.VMEM),
        out_shape=pltpu.VMEM((pairs * bwidth, 1, LANES), jnp.float32),
        scratch_shapes=[
            pltpu.VMEM((bwidth, tile, virt), jnp.float32),
            pltpu.VMEM((pairs * bwidth, LANES), jnp.float32),
        ],
        name="contract",
    )(
        pltpu.with_memory_space_constraint(amplitudes, pltpu.VMEM),
        pltpu.with_memory_space_constraint(pieces, pltpu.VMEM),
    )


def finish_kernel(shares, out):
    out[...] = jnp.sum(shares[:, 0, :], axis=0, keepdims=True)


def finish(shares):
    return pl.pallas_call(
        finish_kernel,
        in_specs=[pl.BlockSpec(memory_space=pltpu.VMEM)],
        out_specs=pl.BlockSpec(memory_space=pltpu.VMEM),
        out_shape=pltpu.VMEM((1, shares.shape[2]), jnp.float32),
        name="finish",
    )(pltpu.with_memory_space_constraint(shares, pltpu.VMEM))


def exchanged(rows, axis, groups=None):
    count = len(groups[0]) if groups else lax.axis_size(axis)
    tiles = rows.reshape(count, rows.shape[0] // (2 * count), 2, LANES)
    tiles = lax.all_to_all(
        tiles, axis, split_axis=0, concat_axis=0, tiled=True, axis_index_groups=groups
    )
    return tiles.reshape(rows.shape)


def on_device(left_factor, right_factor, amplitudes, heights, owner_map, row_site):
    naux, bwidth, dpiece = right_factor.shape
    cols = bwidth * dpiece
    rows = left_factor.shape[0]
    tile = amplitudes.shape[1]
    formers = lax.axis_size("cd")
    parts = lax.axis_size("ij")
    planes = formers // (CORES * SIDE)
    at = [
        [[(s * planes + z) * CORES + c for c in range(CORES)] for z in range(planes)]
        for s in range(SIDE)
    ]
    beside = [[at[s][z][c] for s in range(SIDE) for c in range(CORES)] for z in range(planes)]
    order = plane_order(planes)
    along = [[at[s][z][c] for z in order] for s in range(SIDE) for c in range(CORES)]
    across = [[2 * pair + half for pair in part_order(parts // 2) for half in (1, 0)]]
    place = lax.axis_index("cd").astype(jnp.int32).reshape(1)
    right = jnp.transpose(right_factor, (1, 2, 0)).reshape(cols, naux)
    message = form(
        heights, place, owner_map.reshape(1, rows), row_site, left_factor, right, formers
    )
    arrived = exchanged(message, "cd", beside)
    collated = collate(arrived, planes, tile, cols)
    planar = exchanged(collated, "cd", along)
    coded = combine(planar, planes, parts, tile, cols)
    pieces = exchanged(coded, "ij", across)
    partial = contract(amplitudes, pieces, parts, bwidth)
    shares = lax.all_to_all(
        partial,
        "cd",
        split_axis=0,
        concat_axis=0,
        tiled=True,
        axis_index_groups=[last_order(formers)],
    )
    return finish(shares)[0, :1]


def solution(mesh):
    placed = (
        P("cd", None),
        P(None, None, "ij"),
        P("ij", "cd", None),
        P("cd"),
        P("cd", None, None),
        P("cd", None),
    )
    return jax.shard_map(
        on_device, mesh=mesh, in_specs=placed, out_specs=P(("ij", "cd")), check_vma=False
    )
```
